32 devices in a mesh: groups: 2 (over y), seq: 16 (over z, x, core).
Axes of the slice: x: 2, y: 2, z: 4, core: 2. Of those that a mesh axis runs over, the one named last changes fastest.
Arguments:
- tokens: bfloat16 [4096, 256], P(('groups', 'seq')), parts along dimension 0, may hold values from -6 to 6
- inv_rms_a: float32 [4096], P(('groups', 'seq')), parts along dimension 0, may hold values from 0.5 to 2
- gain_a: float32 [256], replicated, may hold values from 0.1 to 1.9
- proj_a: bfloat16 [256, 768], replicated, may hold values from -0.375 to 0.375
- taps_a: bfloat16 [128, 256], replicated, may hold values from -0.5 to 0.5
- out_a: bfloat16 [256, 256], replicated, may hold values from -0.375 to 0.375
- inv_rms_b: float32 [4096], P(('groups', 'seq')), parts along dimension 0, may hold values from 0.5 to 2
- gain_b: float32 [256], replicated, may hold values from 0.1 to 1.9
- proj_b: bfloat16 [256, 768], replicated, may hold values from -0.375 to 0.375
- rates_b: float32 [16, 256], replicated, may hold values from 1.4648438e-06 to 0.033
- residues_b: float32 [16, 256], replicated, may hold values from -4 to 4
- out_b: bfloat16 [256, 256], replicated, may hold values from -0.375 to 0.375
Outputs:
- partial_a: bfloat16 [4096, 256], P(('groups', 'seq')), parts along dimension 0
- partial_b: bfloat16 [4096, 256], P(('groups', 'seq')), parts along dimension 0
The draws below stay inside these ranges and needn't reach their ends.
There are 2 independent parts, one for each index of `groups`. The reference program is written for one: setup_inputs(seed, part) draws one part's arguments, and reference() takes and returns one part's arrays. A program takes and returns all parts, laid end to end along the dimension named above; an argument that names none is the same for every part. Nothing has to cross between parts.
All inputs are finite; a program needn't handle non-finite values.
Results may differ from the reference program's by a relative error of at most 0.019.
Values may be sent and summed in bfloat16 or wider, within the bound.
A program may use at most 64 MiB of HBM per device.

```python
import math
import jax
import jax.numpy as jnp
from jax import lax

D = 256
TAPS = 128
MODES = 16
TOKENS = 2048


def block_levels(rng, shape, cuts, least, high):
    def one(position, shards_of):
        draws = jax.random.uniform(jax.random.fold_in(jax.random.fold_in(rng, 6), position), (shards_of,), jnp.float32, least / len(cuts), high / len(cuts))
        return jnp.repeat(jnp.exp(draws), shape[position] // shards_of).reshape((-1,) + (1,) * (len(shape) - position - 1))

    level = one(*cuts[0])
    for cut in cuts[1:]:
        level = level * one(*cut)
    return level


def noise(own_key, shape, deviation, most, split=(), kind=jnp.bfloat16):
    result = jax.random.normal(own_key, shape, jnp.float32) * deviation
    if len(split) > 0:
        result = block_levels(own_key, shape, split, -0.22, 0.18) * result
    return jnp.clip(result, min=-most, max=most).astype(kind)


def setup_inputs(seed: int = 0, part: int = 0) -> dict:
    key_list = jax.random.split(jax.random.key(seed), 13)
    part_splits = jax.random.split(jax.random.fold_in(key_list[12], part), 13)
    return {
        "tokens": noise(part_splits[0], (TOKENS, D), 1.0, 6.0, ((0, 16),)),
        "inv_rms_a": jnp.clip(jnp.exp(math.log(2.0) - 1.3862944 * jax.random.uniform(part_splits[1], (TOKENS,), jnp.float32) ** block_levels(part_splits[1], (TOKENS,), ((0, 16),), -0.2, 0.2)), 0.5, 2.0),
        "gain_a": jnp.clip(1.0 + 0.18 * jax.random.normal(key_list[2], (D,), jnp.float32), 0.1, 1.9),
        "proj_a": noise(key_list[3], (D, 3 * D), D ** -0.5, 0.375),
        "taps_a": noise(key_list[4], (TAPS, D), TAPS ** -0.5, 0.5),
        "out_a": noise(key_list[5], (D, D), D ** -0.5, 0.375),
        "inv_rms_b": jnp.clip(jnp.exp(math.log(2.0) - 1.3862944 * jax.random.uniform(part_splits[6], (TOKENS,), jnp.float32) ** block_levels(part_splits[6], (TOKENS,), ((0, 16),), -0.2, 0.2)), 0.5, 2.0),
        "gain_b": jnp.clip(1.0 + 0.18 * jax.random.normal(key_list[7], (D,), jnp.float32), 0.1, 1.9),
        "proj_b": noise(key_list[8], (D, 3 * D), D ** -0.5, 0.375),
        "rates_b": jnp.clip(jnp.exp(jax.random.uniform(key_list[9], (MODES, D), jnp.float32, math.log(1.4648437627329258e-06), math.log(0.033))), 1.4648437627329258e-06, 0.033),
        "residues_b": noise(key_list[10], (MODES, D), 0.3, 4.0, (), jnp.float32),
        "out_b": noise(key_list[11], (D, D), D ** -0.5, 0.375),
    }


HIGHEST_PREC = lax.Precision.HIGHEST

def rms_scale(values, inv_rms, gain):
    floats = values.astype(jnp.float32)
    return (floats * inv_rms[:, None] * gain).astype(jnp.bfloat16)

def mode_weights(rates, residues, length):
    energy = -jnp.expm1(-2.0 * rates) / -jnp.expm1(-2.0 * rates * length)
    return residues * jnp.sqrt(energy)

def long_filter(rates, residues):
    weights = mode_weights(rates, residues, float(TOKENS))
    positions = jnp.arange(TOKENS).astype(jnp.float32)[:, None]

    def add_mode(totals, mode_pair):
        mode_rate, mode_weight = mode_pair
        return (totals + mode_weight[None, :] * jnp.exp(-mode_rate[None, :] * positions), None)
    return lax.scan(add_mode, jnp.zeros((TOKENS, D), jnp.float32), (rates, weights))[0]

def reference(tokens, inv_rms_a, gain_a, proj_a, taps_a, out_a, inv_rms_b, gain_b, proj_b, rates_b, residues_b, out_b):
    normed = rms_scale(tokens, inv_rms_a, gain_a)
    projected = jnp.dot(normed, proj_a, preferred_element_type=jnp.float32)
    queries = projected[:, :D]
    product = (projected[:, D:2 * D] * projected[:, 2 * D:]).astype(jnp.bfloat16)
    kernel = jnp.flip(taps_a.astype(jnp.float32), 0).T[:, None, :]
    signal_in = product.astype(jnp.float32).T[None]
    short_out = lax.conv_general_dilated(signal_in, kernel, (1,), [(TAPS - 1, 0)], dimension_numbers=('NCH', 'OIH', 'NCH'), feature_group_count=D, precision=HIGHEST_PREC)[0].T
    gated_a = (queries * short_out).astype(jnp.bfloat16)
    partial_a = jnp.dot(gated_a, out_a, preferred_element_type=jnp.float32).astype(jnp.bfloat16)
    hidden = (tokens.astype(jnp.float32) + partial_a.astype(jnp.float32)).astype(jnp.bfloat16)
    normed_b = rms_scale(hidden, inv_rms_b, gain_b)
    projected_b = jnp.dot(normed_b, proj_b, preferred_element_type=jnp.float32)
    queries_b = projected_b[:, :D]
    signal = (projected_b[:, D:2 * D] * projected_b[:, 2 * D:]).astype(jnp.bfloat16)
    fft_size = 2 * TOKENS
    spectrum = jnp.fft.rfft(signal.astype(jnp.float32), n=fft_size, axis=0) * jnp.fft.rfft(long_filter(rates_b, residues_b), n=fft_size, axis=0)
    long_out = jnp.fft.irfft(spectrum, n=fft_size, axis=0)[:TOKENS].astype(jnp.bfloat16)
    long_out = lax.optimization_barrier(long_out)
    gated_b = (queries_b * long_out.astype(jnp.float32)).astype(jnp.bfloat16)
    partial_b = jnp.dot(gated_b, out_b, preferred_element_type=jnp.float32).astype(jnp.bfloat16)
    return (partial_a, partial_b)
```

```python
import functools

import jax
import jax.numpy as jnp
import numpy as np
from jax import lax
from jax.experimental import pallas as pl
from jax.experimental.pallas import tpu as pltpu
from jax.sharding import PartitionSpec as P

MESH = pl.DeviceIdType.MESH
F32 = jnp.float32
BF16 = jnp.bfloat16
SUB = 8
LANES = 128


def dft_tables(rows):
    freq = (np.arange(rows) + 0.5)[:, None]
    angle = freq * np.arange(rows)[None, :] * (np.pi / rows)
    cos, sin = np.cos(angle), np.sin(angle)
    sign = np.where(np.arange(rows) % 2 == 0, 1.0, -1.0)[:, None]
    own = np.concatenate([cos, sin], 0)
    behind = np.concatenate([sign * sin, -sign * cos], 0)
    back = own.T / rows
    return [jnp.asarray(t, F32).astype(BF16) for t in (own, behind, back)]


def dot(left, right):
    return jnp.dot(left, right, preferred_element_type=F32)


def split(value):
    high = value.astype(BF16)
    return high, (value - high.astype(F32)).astype(BF16)


def one_minus_exp(a):
    series = 1.0 - a / 9.0
    for k in (8.0, 7.0, 6.0, 5.0, 4.0, 3.0, 2.0):
        series = 1.0 - series * a / k
    return jnp.where(a < 0.5, a * series, 1.0 - jnp.exp(-a))


def column(row):
    rows = row.shape[1]
    eye = lax.broadcasted_iota(jnp.int32, (rows, rows), 0) == lax.broadcasted_iota(
        jnp.int32, (rows, rows), 1
    )
    return jnp.sum(jnp.where(eye, row, 0.0), axis=1, keepdims=True)


def scaled(tokens, scale, gain):
    return (tokens.astype(F32) * scale * gain).astype(BF16)


def spectral_product(data, filt):
    half = data.shape[0] // 2
    dc, ds, fc, fs = data[:half], data[half:], filt[:half], filt[half:]
    return jnp.concatenate([dc * fc - ds * fs, dc * fs + ds * fc], 0).astype(BF16)


def modes_over_rows(first, step, out_ref):
    rows, width = out_ref.shape
    for lane in range(0, width, LANES):
        cols = slice(lane, lane + LANES)
        term, ratio = first[:, :, cols], step[:, :, cols]
        for a in range(rows // SUB):
            out_ref[a * SUB : (a + 1) * SUB, cols] = jnp.sum(term, axis=0)
            if a + 1 < rows // SUB:
                term = term * ratio


def end_state(signal_ref, step, last):
    rows, width = signal_ref.shape
    parts = []
    for lane in range(0, width, LANES):
        cols = slice(lane, lane + LANES)
        ratio = step[:, :, cols]
        total = jnp.broadcast_to(signal_ref[0:SUB, cols][None], ratio.shape)
        for a in range(1, rows // SUB):
            total = total * ratio + signal_ref[a * SUB : (a + 1) * SUB, cols][None]
        parts.append(jnp.sum(total * last[:, :, cols], axis=1))
    return jnp.concatenate(parts, 1)


def kernel(n, *refs):
    hbm = refs[:15]
    pa_ref, pb_ref = refs[15:17]
    vm = refs[17:32]
    (rim_ref, rim_rms_ref, filt_ref, signal_ref, carry_ref, state_ref, states_ref) = refs[32:39]
    (load_sem, rim_send, rim_recv, st_send, st_recv, out_sem, oa_ref, ob_ref) = refs[39:]
    me = lax.axis_index("seq")
    rows, width = vm[0].shape
    modes = vm[9].shape[0]

    barrier = pltpu.get_barrier_semaphore()

    @pl.loop(1, n)
    def _(i):
        pl.semaphore_signal(
            barrier, inc=1, device_id={"seq": lax.rem(me + i, n)}, device_id_type=MESH
        )

    loads = [pltpu.make_async_copy(h, v, load_sem.at[i]) for i, (h, v) in enumerate(zip(hbm, vm))]
    order = (0, 1, 2, 3, 12, 4, 9, 10, 13, 14, 5, 6, 7, 8, 11)
    for i in order:
        loads[i].start()
    (tok, rms_a, gain_a, proj_a, taps, out_a) = vm[:6]
    (rms_b, gain_b, proj_b, rates_ref, resid_ref, out_b, own_f, rim_f, back_f) = vm[6:]

    pl.semaphore_wait(barrier, n - 1)

    def rim_copies():
        target = {"seq": lax.rem(me + 1, n)}
        return [
            pltpu.make_async_remote_copy(
                src_ref=src,
                dst_ref=dst,
                send_sem=rim_send.at[i],
                recv_sem=rim_recv.at[i],
                device_id=target,
                device_id_type=MESH,
            )
            for i, (src, dst) in enumerate(((hbm[0], rim_ref), (hbm[1], rim_rms_ref)))
        ]

    @pl.when(me < n - 1)
    def _():
        for copy in rim_copies():
            copy.start()

    for i in (0, 1, 2, 3):
        loads[i].wait()
    normed = scaled(tok[...], column(rms_a[...]), gain_a[...])
    projected = dot(normed, proj_a[...])
    queries = projected[:, :width]
    product = (projected[:, width : 2 * width] * projected[:, 2 * width :]).astype(BF16)
    loads[12].wait()
    loads[4].wait()
    spectrum = dot(own_f[...], product)
    taps_spec = dot(own_f[...], taps[...])

    loads[9].wait()
    loads[10].wait()
    rates = rates_ref[...]
    length = float(n * rows)
    weights = resid_ref[...] * jnp.sqrt(
        one_minus_exp(2.0 * rates) / one_minus_exp(2.0 * rates * length)
    )
    rates3 = jnp.broadcast_to(rates[:, None, :], (modes, SUB, width))
    within = lax.broadcasted_iota(jnp.int32, (modes, SUB, width), 1).astype(F32)
    step = jnp.exp(-rates3 * float(SUB))
    lag = jnp.exp(-rates3 * within)
    last = jnp.exp(-rates3 * (SUB - 1.0 - within))
    read = jnp.exp(-rates3 * (within + 1.0))
    block = jnp.exp(-rates * float(rows))
    modes_over_rows(weights[:, None, :] * lag, step, filt_ref)
    high, low = split(filt_ref[...])
    long_spec = dot(own_f[...], high) + dot(own_f[...], low)
    for i in (13, 14, 5, 6, 7, 8, 11):
        loads[i].wait()
    scale_b = column(rms_b[...])

    @pl.when(me > 0)
    def _():
        for copy in rim_copies():
            copy.wait_recv()
        rim_normed = scaled(rim_ref[...], column(rim_rms_ref[...]), gain_a[...])
        pair = dot(rim_normed, proj_a[:, width:])
        rim_product = (pair[:, :width] * pair[:, width:]).astype(BF16)
        carry_ref[...] = dot(rim_f[...], rim_product)

    @pl.when(me == 0)
    def _():
        carry_ref[...] = jnp.zeros_like(carry_ref)

    short_out = dot(back_f[...], spectral_product(spectrum + carry_ref[...], taps_spec))
    gated_a = (queries * short_out).astype(BF16)
    partial_a = dot(gated_a, out_a[...]).astype(BF16)
    oa_ref[...] = partial_a
    copy_a = pltpu.make_async_copy(oa_ref, pa_ref, out_sem.at[0])
    copy_a.start()
    hidden = (tok[...].astype(F32) + partial_a.astype(F32)).astype(BF16)
    normed_b = scaled(hidden, scale_b, gain_b[...])
    pair_b = dot(normed_b, proj_b[:, width:])
    signal = (pair_b[:, :width] * pair_b[:, width:]).astype(BF16)
    signal_ref[...] = signal.astype(F32)
    state_ref[...] = end_state(signal_ref, step, last).astype(BF16)

    def state_copy(source, target):
        return pltpu.make_async_remote_copy(
            src_ref=state_ref,
            dst_ref=states_ref.at[source],
            send_sem=st_send.at[target],
            recv_sem=st_recv.at[source],
            device_id={"seq": target},
            device_id_type=MESH,
        )

    @pl.loop(0, n - 1 - me)
    def _(i):
        state_copy(me, n - 1 - i).start()

    queries_b = dot(normed_b, proj_b[:, :width])
    local = dot(back_f[...], spectral_product(dot(own_f[...], signal), long_spec))

    def gather(source, total):
        state_copy(source, lax.rem(me + 1, n)).wait_recv()
        return total * block + states_ref[source].astype(F32)

    total = lax.fori_loop(0, me, gather, jnp.zeros((modes, width), F32))
    modes_over_rows((total * weights)[:, None, :] * read, step, filt_ref)
    long_out = (local + filt_ref[...]).astype(BF16)
    gated_b = (queries_b * long_out.astype(F32)).astype(BF16)
    ob_ref[...] = dot(gated_b, out_b[...]).astype(BF16)
    copy_b = pltpu.make_async_copy(ob_ref, pb_ref, out_sem.at[1])
    copy_b.start()

    @pl.when(me < n - 1)
    def _():
        for copy in rim_copies():
            copy.wait_send()

    @pl.loop(0, n - 1 - me)
    def _(i):
        state_copy(me, n - 1 - i).wait_send()

    copy_a.wait()
    copy_b.wait()


def solution(mesh):
    n = mesh.shape["seq"]

    def on_device(*args):
        rows, width = args[0].shape
        modes = args[9].shape[0]
        args = [a[None] if a.ndim == 1 else a for a in args] + dft_tables(rows)
        block = jax.ShapeDtypeStruct((rows, width), BF16)
        anywhere = pl.BlockSpec(memory_space=pl.ANY)
        return pl.pallas_call(
            functools.partial(kernel, n),
            out_shape=(block, block),
            in_specs=[anywhere] * len(args),
            out_specs=(anywhere, anywhere),
            scratch_shapes=[pltpu.VMEM(a.shape, a.dtype) for a in args]
            + [
                pltpu.VMEM((rows, width), BF16),
                pltpu.VMEM((1, rows), F32),
                pltpu.VMEM((rows, width), F32),
                pltpu.VMEM((rows, width), F32),
                pltpu.VMEM((2 * rows, width), F32),
                pltpu.VMEM((modes, width), BF16),
                pltpu.VMEM((n, modes, width), BF16),
                pltpu.SemaphoreType.DMA((len(args),)),
                pltpu.SemaphoreType.DMA((2,)),
                pltpu.SemaphoreType.DMA((2,)),
                pltpu.SemaphoreType.DMA((n,)),
                pltpu.SemaphoreType.DMA((n,)),
                pltpu.SemaphoreType.DMA((2,)),
                pltpu.VMEM((rows, width), BF16),
                pltpu.VMEM((rows, width), BF16),
            ],
            compiler_params=pltpu.CompilerParams(collective_id=0, has_side_effects=True),
        )(*args)

    shard = P(("groups", "seq"))
    wide = P(("groups", "seq"), None)
    placed = (wide, shard, P(), P(), P(), P(), shard, P(), P(), P(), P(), P())
    return jax.shard_map(
        on_device, mesh=mesh, in_specs=placed, out_specs=(wide, wide), check_vma=False
    )
```

```python
import functools

import jax
import jax.numpy as jnp
import numpy as np
from jax import lax
from jax.experimental import pallas as pl
from jax.experimental.pallas import tpu as pltpu
from jax.sharding import PartitionSpec as P

MESH = pl.DeviceIdType.MESH
F32 = jnp.float32
BF16 = jnp.bfloat16
SUB = 8
LANES = 128


def dft_tables(rows):
    freq = (np.arange(rows) + 0.5)[:, None]
    angle = freq * np.arange(rows)[None, :] * (np.pi / rows)
    cos, sin = np.cos(angle), np.sin(angle)
    sign = np.where(np.arange(rows) % 2 == 0, 1.0, -1.0)[:, None]
    own = np.concatenate([cos, sin], 0)
    behind = np.concatenate([sign * sin, -sign * cos], 0)
    back = own.T / rows
    return [jnp.asarray(t, F32).astype(BF16) for t in (own, behind, back)]


def dot(left, right):
    return jnp.dot(left, right, preferred_element_type=F32)


def split(value):
    high = value.astype(BF16)
    return high, (value - high.astype(F32)).astype(BF16)


def one_minus_exp(a):
    series = 1.0 - a / 9.0
    for k in (8.0, 7.0, 6.0, 5.0, 4.0, 3.0, 2.0):
        series = 1.0 - series * a / k
    return jnp.where(a < 0.5, a * series, 1.0 - jnp.exp(-a))


def column(row):
    rows = row.shape[1]
    eye = lax.broadcasted_iota(jnp.int32, (rows, rows), 0) == lax.broadcasted_iota(
        jnp.int32, (rows, rows), 1
    )
    return jnp.sum(jnp.where(eye, row, 0.0), axis=1, keepdims=True)


def scaled(tokens, scale, gain):
    return (tokens.astype(F32) * scale * gain).astype(BF16)


def spectral_product(data, filt):
    half = data.shape[0] // 2
    dc, ds, fc, fs = data[:half], data[half:], filt[:half], filt[half:]
    return jnp.concatenate([dc * fc - ds * fs, dc * fs + ds * fc], 0).astype(BF16)


def modes_over_rows(first, step, out_ref):
    rows, width = out_ref.shape
    for lane in range(0, width, LANES):
        cols = slice(lane, lane + LANES)
        term, ratio = first[:, :, cols], step[:, :, cols]
        for a in range(rows // SUB):
            out_ref[a * SUB : (a + 1) * SUB, cols] = jnp.sum(term, axis=0)
            if a + 1 < rows // SUB:
                term = term * ratio


def end_state(signal_ref, step, last):
    rows, width = signal_ref.shape
    parts = []
    for lane in range(0, width, LANES):
        cols = slice(lane, lane + LANES)
        ratio = step[:, :, cols]
        total = jnp.broadcast_to(signal_ref[0:SUB, cols][None], ratio.shape)
        for a in range(1, rows // SUB):
            total = total * ratio + signal_ref[a * SUB : (a + 1) * SUB, cols][None]
        parts.append(jnp.sum(total * last[:, :, cols], axis=1))
    return jnp.concatenate(parts, 1)


def plane_size(n):
    size = 1
    while n % (2 * size) == 0 and 4 * size * size <= n:
        size *= 2
    return size


def hand_out(a_ref, b_ref, pa_ref, pb_ref, sem):
    copies = [
        pltpu.make_async_copy(a_ref, pa_ref, sem.at[0]),
        pltpu.make_async_copy(b_ref, pb_ref, sem.at[1]),
    ]
    for copy in copies:
        copy.start()
    for copy in copies:
        copy.wait()


def kernel(n, *refs):
    hbm = refs[:15]
    pa_ref, pb_ref = refs[15:17]
    vm = refs[17:32]
    (rim_ref, rim_rms_ref, filt_ref, signal_ref, carry_ref, state_ref, states_ref) = refs[32:39]
    (load_sem, rim_send, rim_recv, st_send, st_recv, far_sem) = refs[39:]
    me = lax.axis_index("seq")
    rows, width = vm[0].shape
    modes = vm[9].shape[0]

    plane = plane_size(n)
    planes = n // plane
    level, place = me // plane, lax.rem(me, plane)
    barrier = pltpu.get_barrier_semaphore()

    def signal(sem, target):
        pl.semaphore_signal(sem, inc=1, device_id={"seq": target}, device_id_type=MESH)

    @pl.loop(1, plane)
    def _(i):
        signal(barrier, level * plane + lax.rem(place + i, plane))

    @pl.loop(level + 1, planes)
    def _(i):
        signal(barrier, i * plane + place)

    @pl.when(jnp.logical_and(place == 0, level > 0))
    def _():
        signal(barrier, me - 1)

    loads = [pltpu.make_async_copy(h, v, load_sem.at[i]) for i, (h, v) in enumerate(zip(hbm, vm))]
    order = (0, 1, 2, 3, 12, 4, 9, 10, 13, 14, 5, 6, 7, 8, 11)
    for i in order:
        loads[i].start()
    (tok, rms_a, gain_a, proj_a, taps, out_a) = vm[:6]
    (rms_b, gain_b, proj_b, rates_ref, resid_ref, out_b, own_f, rim_f, back_f) = vm[6:]

    crossing = jnp.logical_and(place == plane - 1, level < planes - 1)
    pl.semaphore_wait(barrier, plane - 1 + level + crossing.astype(jnp.int32))

    def rim_copies():
        target = {"seq": lax.rem(me + 1, n)}
        return [
            pltpu.make_async_remote_copy(
                src_ref=src,
                dst_ref=dst,
                send_sem=rim_send.at[i],
                recv_sem=rim_recv.at[i],
                device_id=target,
                device_id_type=MESH,
            )
            for i, (src, dst) in enumerate(((hbm[0], rim_ref), (hbm[1], rim_rms_ref)))
        ]

    @pl.when(me < n - 1)
    def _():
        for copy in rim_copies():
            copy.start()

    @pl.loop(0, level)
    def _(i):
        signal(far_sem, i * plane + place)

    for i in (0, 1, 2, 3):
        loads[i].wait()
    normed = scaled(tok[...], column(rms_a[...]), gain_a[...])
    projected = dot(normed, proj_a[...])
    queries = projected[:, :width]
    product = (projected[:, width : 2 * width] * projected[:, 2 * width :]).astype(BF16)
    loads[12].wait()
    loads[4].wait()
    spectrum = dot(own_f[...], product)
    taps_spec = dot(own_f[...], taps[...])

    loads[9].wait()
    loads[10].wait()
    rates = rates_ref[...]
    length = float(n * rows)
    weights = resid_ref[...] * jnp.sqrt(
        one_minus_exp(2.0 * rates) / one_minus_exp(2.0 * rates * length)
    )
    rates3 = jnp.broadcast_to(rates[:, None, :], (modes, SUB, width))
    within = lax.broadcasted_iota(jnp.int32, (modes, SUB, width), 1).astype(F32)
    step = jnp.exp(-rates3 * float(SUB))
    lag = jnp.exp(-rates3 * within)
    last = jnp.exp(-rates3 * (SUB - 1.0 - within))
    read = jnp.exp(-rates3 * (within + 1.0))
    block = jnp.exp(-rates * float(rows))
    modes_over_rows(weights[:, None, :] * lag, step, filt_ref)
    high, low = split(filt_ref[...])
    long_spec = dot(own_f[...], high) + dot(own_f[...], low)
    for i in (13, 14, 5, 6, 7, 8, 11):
        loads[i].wait()
    scale_b = column(rms_b[...])

    @pl.when(me > 0)
    def _():
        for copy in rim_copies():
            copy.wait_recv()
        rim_normed = scaled(rim_ref[...], column(rim_rms_ref[...]), gain_a[...])
        pair = dot(rim_normed, proj_a[:, width:])
        rim_product = (pair[:, :width] * pair[:, width:]).astype(BF16)
        carry_ref[...] = dot(rim_f[...], rim_product)

    @pl.when(me == 0)
    def _():
        carry_ref[...] = jnp.zeros_like(carry_ref)

    short_out = dot(back_f[...], spectral_product(spectrum + carry_ref[...], taps_spec))
    gated_a = (queries * short_out).astype(BF16)
    partial_a = dot(gated_a, out_a[...]).astype(BF16)
    pa_ref[...] = partial_a
    hidden = (tok[...].astype(F32) + partial_a.astype(F32)).astype(BF16)
    normed_b = scaled(hidden, scale_b, gain_b[...])
    pair_b = dot(normed_b, proj_b[:, width:])
    signal = (pair_b[:, :width] * pair_b[:, width:]).astype(BF16)
    signal_ref[...] = signal.astype(F32)
    state_ref[...] = end_state(signal_ref, step, last).astype(BF16)

    def state_copy(source, target):
        return pltpu.make_async_remote_copy(
            src_ref=state_ref,
            dst_ref=states_ref.at[source],
            send_sem=st_send.at[target],
            recv_sem=st_recv.at[source],
            device_id={"seq": target},
            device_id_type=MESH,
        )

    @pl.when(level < planes - 1)
    def _():
        pl.semaphore_wait(far_sem, planes - 1 - level)

    @pl.loop(0, n - 1 - me)
    def _(i):
        state_copy(me, n - 1 - i).start()

    queries_b = dot(normed_b, proj_b[:, :width])
    local = dot(back_f[...], spectral_product(dot(own_f[...], signal), long_spec))

    def gather(source, total):
        state_copy(source, lax.rem(me + 1, n)).wait_recv()
        return total * block + states_ref[source].astype(F32)

    total = lax.fori_loop(0, me, gather, jnp.zeros((modes, width), F32))
    modes_over_rows((total * weights)[:, None, :] * read, step, filt_ref)
    long_out = (local + filt_ref[...]).astype(BF16)
    gated_b = (queries_b * long_out.astype(F32)).astype(BF16)
    pb_ref[...] = dot(gated_b, out_b[...]).astype(BF16)

    @pl.when(me < n - 1)
    def _():
        for copy in rim_copies():
            copy.wait_send()

    @pl.loop(0, n - 1 - me)
    def _(i):
        state_copy(me, n - 1 - i).wait_send()


def solution(mesh):
    n = mesh.shape["seq"]

    def on_device(*args):
        rows, width = args[0].shape
        modes = args[9].shape[0]
        args = [a[None] if a.ndim == 1 else a for a in args] + dft_tables(rows)
        block = jax.ShapeDtypeStruct((rows, width), BF16)
        fast = pltpu.VMEM((rows, width), BF16)
        inside = pl.BlockSpec(memory_space=pltpu.VMEM)
        anywhere = pl.BlockSpec(memory_space=pl.ANY)
        results = pl.pallas_call(
            functools.partial(kernel, n),
            out_shape=(fast, fast),
            in_specs=[anywhere] * len(args),
            out_specs=(inside, inside),
            scratch_shapes=[pltpu.VMEM(a.shape, a.dtype) for a in args]
            + [
                pltpu.VMEM((rows, width), BF16),
                pltpu.VMEM((1, rows), F32),
                pltpu.VMEM((rows, width), F32),
                pltpu.VMEM((rows, width), F32),
                pltpu.VMEM((2 * rows, width), F32),
                pltpu.VMEM((modes, width), BF16),
                pltpu.VMEM((n, modes, width), BF16),
                pltpu.SemaphoreType.DMA((len(args),)),
                pltpu.SemaphoreType.DMA((2,)),
                pltpu.SemaphoreType.DMA((2,)),
                pltpu.SemaphoreType.DMA((n,)),
                pltpu.SemaphoreType.DMA((n,)),
                pltpu.SemaphoreType.REGULAR,
            ],
            compiler_params=pltpu.CompilerParams(collective_id=0, has_side_effects=True),
        )(*args)
        return pl.pallas_call(
            hand_out,
            out_shape=(block, block),
            in_specs=[inside] * 2,
            out_specs=(anywhere, anywhere),
            scratch_shapes=[pltpu.SemaphoreType.DMA((2,))],
        )(*[pltpu.with_memory_space_constraint(r, pltpu.VMEM) for r in results])

    shard = P(("groups", "seq"))
    wide = P(("groups", "seq"), None)
    placed = (wide, shard, P(), P(), P(), P(), shard, P(), P(), P(), P(), P())
    return jax.shard_map(
        on_device, mesh=mesh, in_specs=placed, out_specs=(wide, wide), check_vma=False
    )
```

```python
import functools

import jax
import jax.numpy as jnp
import numpy as np
from jax import lax
from jax.experimental import pallas as pl
from jax.experimental.pallas import tpu as pltpu
from jax.sharding import PartitionSpec as P

MESH = pl.DeviceIdType.MESH
F32 = jnp.float32
BF16 = jnp.bfloat16
SUB = 8
LANES = 128


def dft_tables(rows):
    freq = (np.arange(rows) + 0.5)[:, None]
    angle = freq * np.arange(rows)[None, :] * (np.pi / rows)
    cos, sin = np.cos(angle), np.sin(angle)
    sign = np.where(np.arange(rows) % 2 == 0, 1.0, -1.0)[:, None]
    own = np.concatenate([cos, sin], 0)
    behind = np.concatenate([sign * sin, -sign * cos], 0)
    back = own.T / rows
    return [jnp.asarray(t, F32).astype(BF16) for t in (own, behind, back)]


def dot(left, right):
    return jnp.dot(left, right, preferred_element_type=F32)


def split(value):
    high = value.astype(BF16)
    return high, (value - high.astype(F32)).astype(BF16)


def one_minus_exp(a):
    series = 1.0 - a / 9.0
    for k in (8.0, 7.0, 6.0, 5.0, 4.0, 3.0, 2.0):
        series = 1.0 - series * a / k
    return jnp.where(a < 0.5, a * series, 1.0 - jnp.exp(-a))


def column(row):
    rows = row.shape[1]
    eye = lax.broadcasted_iota(jnp.int32, (rows, rows), 0) == lax.broadcasted_iota(
        jnp.int32, (rows, rows), 1
    )
    return jnp.sum(jnp.where(eye, row, 0.0), axis=1, keepdims=True)


def scaled(tokens, scale, gain):
    return (tokens.astype(F32) * scale * gain).astype(BF16)


def spectral_product(data, filt):
    half = data.shape[0] // 2
    dc, ds, fc, fs = data[:half], data[half:], filt[:half], filt[half:]
    return jnp.concatenate([dc * fc - ds * fs, dc * fs + ds * fc], 0).astype(BF16)


def modes_over_rows(first, step, out_ref):
    rows, width = out_ref.shape
    for lane in range(0, width, LANES):
        cols = slice(lane, lane + LANES)
        term, ratio = first[:, :, cols], step[:, :, cols]
        for a in range(rows // SUB):
            out_ref[a * SUB : (a + 1) * SUB, cols] = jnp.sum(term, axis=0)
            if a + 1 < rows // SUB:
                term = term * ratio


def end_state(signal_ref, step, last):
    rows, width = signal_ref.shape
    parts = []
    for lane in range(0, width, LANES):
        cols = slice(lane, lane + LANES)
        ratio = step[:, :, cols]
        total = jnp.broadcast_to(signal_ref[0:SUB, cols][None], ratio.shape)
        for a in range(1, rows // SUB):
            total = total * ratio + signal_ref[a * SUB : (a + 1) * SUB, cols][None]
        parts.append(jnp.sum(total * last[:, :, cols], axis=1))
    return jnp.concatenate(parts, 1)


def plane_size(n):
    size = 1
    while n % (2 * size) == 0 and 4 * size * size <= n:
        size *= 2
    return size


def hand_out(a_ref, b_ref, pa_ref, pb_ref, sem):
    copies = [
        pltpu.make_async_copy(a_ref, pa_ref, sem.at[0]),
        pltpu.make_async_copy(b_ref, pb_ref, sem.at[1]),
    ]
    for copy in copies:
        copy.start()
    for copy in copies:
        copy.wait()


def kernel(n, *refs):
    hbm = refs[:15]
    pa_ref, pb_ref = refs[15:17]
    vm = refs[17:32]
    (product_ref, rim_ref, filt_ref, signal_ref, carry_ref, state_ref, states_ref) = refs[32:39]
    (load_sem, rim_send, rim_recv, st_send, st_recv, far_sem) = refs[39:]
    me = lax.axis_index("seq")
    rows, width = vm[0].shape
    modes = vm[9].shape[0]

    plane = plane_size(n)
    planes = n // plane
    level, place = me // plane, lax.rem(me, plane)
    barrier = pltpu.get_barrier_semaphore()

    def signal(sem, target):
        pl.semaphore_signal(sem, inc=1, device_id={"seq": target}, device_id_type=MESH)

    @pl.loop(1, plane)
    def _(i):
        signal(barrier, level * plane + lax.rem(place + i, plane))

    @pl.loop(level + 1, planes)
    def _(i):
        signal(barrier, i * plane + place)

    @pl.when(jnp.logical_and(place == 0, level > 0))
    def _():
        signal(barrier, me - 1)

    loads = [pltpu.make_async_copy(h, v, load_sem.at[i]) for i, (h, v) in enumerate(zip(hbm, vm))]
    order = (0, 1, 2, 3, 12, 4, 9, 10, 13, 14, 5, 6, 7, 8, 11)
    for i in order:
        loads[i].start()
    (tok, rms_a, gain_a, proj_a, taps, out_a) = vm[:6]
    (rms_b, gain_b, proj_b, rates_ref, resid_ref, out_b, own_f, rim_f, back_f) = vm[6:]

    for i in (0, 1, 2, 3):
        loads[i].wait()
    normed = scaled(tok[...], column(rms_a[...]), gain_a[...])
    projected = dot(normed, proj_a[...])
    queries = projected[:, :width]
    product = (projected[:, width : 2 * width] * projected[:, 2 * width :]).astype(BF16)
    product_ref[...] = product

    crossing = jnp.logical_and(place == plane - 1, level < planes - 1)
    pl.semaphore_wait(barrier, plane - 1 + level + crossing.astype(jnp.int32))

    rim_copy = pltpu.make_async_remote_copy(
        src_ref=product_ref,
        dst_ref=rim_ref,
        send_sem=rim_send,
        recv_sem=rim_recv,
        device_id={"seq": lax.rem(me + 1, n)},
        device_id_type=MESH,
    )

    @pl.when(me < n - 1)
    def _():
        rim_copy.start()

    @pl.loop(0, level)
    def _(i):
        signal(far_sem, i * plane + place)

    loads[12].wait()
    loads[4].wait()
    spectrum = dot(own_f[...], product)
    taps_spec = dot(own_f[...], taps[...])

    loads[9].wait()
    loads[10].wait()
    rates = rates_ref[...]
    length = float(n * rows)
    weights = resid_ref[...] * jnp.sqrt(
        one_minus_exp(2.0 * rates) / one_minus_exp(2.0 * rates * length)
    )
    rates3 = jnp.broadcast_to(rates[:, None, :], (modes, SUB, width))
    within = lax.broadcasted_iota(jnp.int32, (modes, SUB, width), 1).astype(F32)
    step = jnp.exp(-rates3 * float(SUB))
    lag = jnp.exp(-rates3 * within)
    last = jnp.exp(-rates3 * (SUB - 1.0 - within))
    read = jnp.exp(-rates3 * (within + 1.0))
    block = jnp.exp(-rates * float(rows))
    modes_over_rows(weights[:, None, :] * lag, step, filt_ref)
    high, low = split(filt_ref[...])
    long_spec = dot(own_f[...], high) + dot(own_f[...], low)
    for i in (13, 14, 5, 6, 7, 8, 11):
        loads[i].wait()
    scale_b = column(rms_b[...])

    @pl.when(me > 0)
    def _():
        rim_copy.wait_recv()
        carry_ref[...] = dot(rim_f[...], rim_ref[...])

    @pl.when(me == 0)
    def _():
        carry_ref[...] = jnp.zeros_like(carry_ref)

    short_out = dot(back_f[...], spectral_product(spectrum + carry_ref[...], taps_spec))
    gated_a = (queries * short_out).astype(BF16)
    partial_a = dot(gated_a, out_a[...]).astype(BF16)
    pa_ref[...] = partial_a
    hidden = (tok[...].astype(F32) + partial_a.astype(F32)).astype(BF16)
    normed_b = scaled(hidden, scale_b, gain_b[...])
    pair_b = dot(normed_b, proj_b[:, width:])
    signal = (pair_b[:, :width] * pair_b[:, width:]).astype(BF16)
    signal_ref[...] = signal.astype(F32)
    state_ref[...] = end_state(signal_ref, step, last).astype(BF16)

    def state_copy(source, target):
        return pltpu.make_async_remote_copy(
            src_ref=state_ref,
            dst_ref=states_ref.at[source],
            send_sem=st_send.at[target],
            recv_sem=st_recv.at[source],
            device_id={"seq": target},
            device_id_type=MESH,
        )

    @pl.when(level < planes - 1)
    def _():
        pl.semaphore_wait(far_sem, planes - 1 - level)

    @pl.loop(0, n - 1 - me)
    def _(i):
        state_copy(me, n - 1 - i).start()

    queries_b = dot(normed_b, proj_b[:, :width])
    local = dot(back_f[...], spectral_product(dot(own_f[...], signal), long_spec))

    def gather(source, total):
        state_copy(source, lax.rem(me + 1, n)).wait_recv()
        return total * block + states_ref[source].astype(F32)

    total = lax.fori_loop(0, me, gather, jnp.zeros((modes, width), F32))
    modes_over_rows((total * weights)[:, None, :] * read, step, filt_ref)
    long_out = (local + filt_ref[...]).astype(BF16)
    gated_b = (queries_b * long_out.astype(F32)).astype(BF16)
    pb_ref[...] = dot(gated_b, out_b[...]).astype(BF16)

    @pl.when(me < n - 1)
    def _():
        rim_copy.wait_send()

    @pl.loop(0, n - 1 - me)
    def _(i):
        state_copy(me, n - 1 - i).wait_send()


def solution(mesh):
    n = mesh.shape["seq"]

    def on_device(*args):
        rows, width = args[0].shape
        modes = args[9].shape[0]
        args = [a[None] if a.ndim == 1 else a for a in args] + dft_tables(rows)
        block = jax.ShapeDtypeStruct((rows, width), BF16)
        fast = pltpu.VMEM((rows, width), BF16)
        inside = pl.BlockSpec(memory_space=pltpu.VMEM)
        anywhere = pl.BlockSpec(memory_space=pl.ANY)
        results = pl.pallas_call(
            functools.partial(kernel, n),
            out_shape=(fast, fast),
            in_specs=[anywhere] * len(args),
            out_specs=(inside, inside),
            scratch_shapes=[pltpu.VMEM(a.shape, a.dtype) for a in args]
            + [
                pltpu.VMEM((rows, width), BF16),
                pltpu.VMEM((rows, width), BF16),
                pltpu.VMEM((rows, width), F32),
                pltpu.VMEM((rows, width), F32),
                pltpu.VMEM((2 * rows, width), F32),
                pltpu.VMEM((modes, width), BF16),
                pltpu.VMEM((n, modes, width), BF16),
                pltpu.SemaphoreType.DMA((len(args),)),
                pltpu.SemaphoreType.DMA,
                pltpu.SemaphoreType.DMA,
                pltpu.SemaphoreType.DMA((n,)),
                pltpu.SemaphoreType.DMA((n,)),
                pltpu.SemaphoreType.REGULAR,
            ],
            compiler_params=pltpu.CompilerParams(collective_id=0, has_side_effects=True),
        )(*args)
        return pl.pallas_call(
            hand_out,
            out_shape=(block, block),
            in_specs=[inside] * 2,
            out_specs=(anywhere, anywhere),
            scratch_shapes=[pltpu.SemaphoreType.DMA((2,))],
        )(*[pltpu.with_memory_space_constraint(r, pltpu.VMEM) for r in results])

    shard = P(("groups", "seq"))
    wide = P(("groups", "seq"), None)
    placed = (wide, shard, P(), P(), P(), P(), shard, P(), P(), P(), P(), P())
    return jax.shard_map(
        on_device, mesh=mesh, in_specs=placed, out_specs=(wide, wide), check_vma=False
    )
```

```python
import functools

import jax
import jax.numpy as jnp
import numpy as np
from jax import lax
from jax.experimental import pallas as pl
from jax.experimental.pallas import tpu as pltpu
from jax.sharding import PartitionSpec as P

MESH = pl.DeviceIdType.MESH
F32 = jnp.float32
BF16 = jnp.bfloat16
SUB = 8
LANES = 128


def dft_tables(rows):
    freq = (np.arange(rows) + 0.5)[:, None]
    angle = freq * np.arange(rows)[None, :] * (np.pi / rows)
    cos, sin = np.cos(angle), np.sin(angle)
    sign = np.where(np.arange(rows) % 2 == 0, 1.0, -1.0)[:, None]
    own = np.concatenate([cos, sin], 0)
    behind = np.concatenate([sign * sin, -sign * cos], 0)
    back = own.T / rows
    return [jnp.asarray(t, F32).astype(BF16) for t in (own, behind, back)]


def dot(left, right):
    return jnp.dot(left, right, preferred_element_type=F32)


def split(value):
    high = value.astype(BF16)
    return high, (value - high.astype(F32)).astype(BF16)


def one_minus_exp(a):
    series = 1.0 - a / 9.0
    for k in (8.0, 7.0, 6.0, 5.0, 4.0, 3.0, 2.0):
        series = 1.0 - series * a / k
    return jnp.where(a < 0.5, a * series, 1.0 - jnp.exp(-a))


def column(row):
    rows = row.shape[1]
    eye = lax.broadcasted_iota(jnp.int32, (rows, rows), 0) == lax.broadcasted_iota(
        jnp.int32, (rows, rows), 1
    )
    return jnp.sum(jnp.where(eye, row, 0.0), axis=1, keepdims=True)


def scaled(tokens, scale, gain):
    return (tokens.astype(F32) * scale * gain).astype(BF16)


def spectral_product(data, filt):
    half = data.shape[0] // 2
    dc, ds, fc, fs = data[:half], data[half:], filt[:half], filt[half:]
    return jnp.concatenate([dc * fc - ds * fs, dc * fs + ds * fc], 0).astype(BF16)


def modes_over_rows(first, step, out_ref):
    rows, width = out_ref.shape
    for lane in range(0, width, LANES):
        cols = slice(lane, lane + LANES)
        term, ratio = first[:, :, cols], step[:, :, cols]
        for a in range(rows // SUB):
            out_ref[a * SUB : (a + 1) * SUB, cols] = jnp.sum(term, axis=0)
            if a + 1 < rows // SUB:
                term = term * ratio


def end_state(signal_ref, step, last):
    rows, width = signal_ref.shape
    parts = []
    for lane in range(0, width, LANES):
        cols = slice(lane, lane + LANES)
        ratio = step[:, :, cols]
        total = jnp.broadcast_to(signal_ref[0:SUB, cols][None], ratio.shape)
        for a in range(1, rows // SUB):
            total = total * ratio + signal_ref[a * SUB : (a + 1) * SUB, cols][None]
        parts.append(jnp.sum(total * last[:, :, cols], axis=1))
    return jnp.concatenate(parts, 1)


def plane_size(n):
    size = 1
    while n % (2 * size) == 0 and 4 * size * size <= n:
        size *= 2
    return size


def hand_out(a_ref, b_ref, pa_ref, pb_ref, sem):
    copies = [
        pltpu.make_async_copy(a_ref, pa_ref, sem.at[0]),
        pltpu.make_async_copy(b_ref, pb_ref, sem.at[1]),
    ]
    for copy in copies:
        copy.start()
    for copy in copies:
        copy.wait()


def kernel(n, *refs):
    hbm = refs[:15]
    pa_ref, pb_ref = refs[15:17]
    vm = refs[17:32]
    (product_ref, rim_ref, filt_ref, signal_ref, carry_ref, state_ref, states_ref) = refs[32:39]
    (load_sem, rim_send, rim_recv, st_send, st_recv, far_sem) = refs[39:]
    me = lax.axis_index("seq")
    rows, width = vm[0].shape
    modes = vm[9].shape[0]

    plane = plane_size(n)
    planes = n // plane
    level, place = me // plane, lax.rem(me, plane)
    barrier = pltpu.get_barrier_semaphore()

    def signal(sem, target):
        pl.semaphore_signal(sem, inc=1, device_id={"seq": target}, device_id_type=MESH)

    @pl.loop(1, plane)
    def _(i):
        signal(barrier, level * plane + lax.rem(place + i, plane))

    @pl.loop(level + 1, planes)
    def _(i):
        signal(barrier, i * plane + place)

    @pl.when(jnp.logical_and(place == 0, level > 0))
    def _():
        signal(barrier, me - 1)

    loads = [pltpu.make_async_copy(h, v, load_sem.at[i]) for i, (h, v) in enumerate(zip(hbm, vm))]
    order = (0, 1, 2, 3, 12, 4, 9, 10, 13, 14, 5, 6, 7, 8, 11)
    for i in order:
        loads[i].start()
    (tok, rms_a, gain_a, proj_a, taps, out_a) = vm[:6]
    (rms_b, gain_b, proj_b, rates_ref, resid_ref, out_b, own_f, rim_f, back_f) = vm[6:]

    for i in (0, 1, 2, 3):
        loads[i].wait()
    normed = scaled(tok[...], column(rms_a[...]), gain_a[...])
    projected = dot(normed, proj_a[...])
    queries = projected[:, :width]
    product = (projected[:, width : 2 * width] * projected[:, 2 * width :]).astype(BF16)
    product_ref[...] = product

    crossing = jnp.logical_and(place == plane - 1, level < planes - 1)
    pl.semaphore_wait(barrier, plane - 1 + level + crossing.astype(jnp.int32))

    rim_copy = pltpu.make_async_remote_copy(
        src_ref=product_ref,
        dst_ref=rim_ref,
        send_sem=rim_send,
        recv_sem=rim_recv,
        device_id={"seq": lax.rem(me + 1, n)},
        device_id_type=MESH,
    )

    @pl.when(me < n - 1)
    def _():
        rim_copy.start()

    @pl.loop(0, level)
    def _(i):
        signal(far_sem, i * plane + place)

    loads[12].wait()
    loads[4].wait()
    spectrum = dot(own_f[...], product)
    taps_spec = dot(own_f[...], taps[...])

    loads[9].wait()
    loads[10].wait()
    rates = rates_ref[...]
    length = float(n * rows)
    weights = resid_ref[...] * jnp.sqrt(
        one_minus_exp(2.0 * rates) / one_minus_exp(2.0 * rates * length)
    )
    rates3 = jnp.broadcast_to(rates[:, None, :], (modes, SUB, width))
    within = lax.broadcasted_iota(jnp.int32, (modes, SUB, width), 1).astype(F32)
    step = jnp.exp(-rates3 * float(SUB))
    lag = jnp.exp(-rates3 * within)
    last = jnp.exp(-rates3 * (SUB - 1.0 - within))
    read = jnp.exp(-rates3 * (within + 1.0))
    block = jnp.exp(-rates * float(rows))
    modes_over_rows(weights[:, None, :] * lag, step, filt_ref)
    high, low = split(filt_ref[...])
    long_spec = dot(own_f[...], high) + dot(own_f[...], low)
    for i in (13, 14, 5, 6, 7, 8, 11):
        loads[i].wait()
    scale_b = column(rms_b[...])

    @pl.when(me > 0)
    def _():
        rim_copy.wait_recv()
        carry_ref[...] = dot(rim_f[...], rim_ref[...])

    @pl.when(me == 0)
    def _():
        carry_ref[...] = jnp.zeros_like(carry_ref)

    short_out = dot(back_f[...], spectral_product(spectrum + carry_ref[...], taps_spec))
    gated_a = (queries * short_out).astype(BF16)
    partial_a = dot(gated_a, out_a[...]).astype(BF16)
    pa_ref[...] = partial_a
    hidden = (tok[...].astype(F32) + partial_a.astype(F32)).astype(BF16)
    normed_b = scaled(hidden, scale_b, gain_b[...])
    pair_b = dot(normed_b, proj_b[:, width:])
    signal = (pair_b[:, :width] * pair_b[:, width:]).astype(BF16)
    signal_ref[...] = signal.astype(F32)
    state_ref[...] = end_state(signal_ref, step, last).astype(BF16)

    def state_copy(source, target):
        return pltpu.make_async_remote_copy(
            src_ref=state_ref,
            dst_ref=states_ref.at[source],
            send_sem=st_send.at[target],
            recv_sem=st_recv.at[source],
            device_id={"seq": target},
            device_id_type=MESH,
        )

    @pl.loop(me + 1, (level + 1) * plane)
    def _(target):
        state_copy(me, target).start()

    @pl.when(level < planes - 1)
    def _():
        pl.semaphore_wait(far_sem, planes - 1 - level)

    @pl.loop(0, plane)
    def _(i):
        @pl.loop(0, planes - 1 - level)
        def _(k):
            state_copy(me, (planes - 1 - k) * plane + i).start()


    queries_b = dot(normed_b, proj_b[:, :width])
    local = dot(back_f[...], spectral_product(dot(own_f[...], signal), long_spec))

    def gather(source, total):
        state_copy(source, lax.rem(me + 1, n)).wait_recv()
        return total * block + states_ref[source].astype(F32)

    total = lax.fori_loop(0, me, gather, jnp.zeros((modes, width), F32))
    modes_over_rows((total * weights)[:, None, :] * read, step, filt_ref)
    long_out = (local + filt_ref[...]).astype(BF16)
    gated_b = (queries_b * long_out.astype(F32)).astype(BF16)
    pb_ref[...] = dot(gated_b, out_b[...]).astype(BF16)

    @pl.when(me < n - 1)
    def _():
        rim_copy.wait_send()

    @pl.loop(0, n - 1 - me)
    def _(i):
        state_copy(me, n - 1 - i).wait_send()


def solution(mesh):
    n = mesh.shape["seq"]

    def on_device(*args):
        rows, width = args[0].shape
        modes = args[9].shape[0]
        args = [a[None] if a.ndim == 1 else a for a in args] + dft_tables(rows)
        block = jax.ShapeDtypeStruct((rows, width), BF16)
        fast = pltpu.VMEM((rows, width), BF16)
        inside = pl.BlockSpec(memory_space=pltpu.VMEM)
        anywhere = pl.BlockSpec(memory_space=pl.ANY)
        results = pl.pallas_call(
            functools.partial(kernel, n),
            out_shape=(fast, fast),
            in_specs=[anywhere] * len(args),
            out_specs=(inside, inside),
            scratch_shapes=[pltpu.VMEM(a.shape, a.dtype) for a in args]
            + [
                pltpu.VMEM((rows, width), BF16),
                pltpu.VMEM((rows, width), BF16),
                pltpu.VMEM((rows, width), F32),
                pltpu.VMEM((rows, width), F32),
                pltpu.VMEM((2 * rows, width), F32),
                pltpu.VMEM((modes, width), BF16),
                pltpu.VMEM((n, modes, width), BF16),
                pltpu.SemaphoreType.DMA((len(args),)),
                pltpu.SemaphoreType.DMA,
                pltpu.SemaphoreType.DMA,
                pltpu.SemaphoreType.DMA((n,)),
                pltpu.SemaphoreType.DMA((n,)),
                pltpu.SemaphoreType.REGULAR,
            ],
            compiler_params=pltpu.CompilerParams(collective_id=0, has_side_effects=True),
        )(*args)
        return pl.pallas_call(
            hand_out,
            out_shape=(block, block),
            in_specs=[inside] * 2,
            out_specs=(anywhere, anywhere),
            scratch_shapes=[pltpu.SemaphoreType.DMA((2,))],
        )(*[pltpu.with_memory_space_constraint(r, pltpu.VMEM) for r in results])

    shard = P(("groups", "seq"))
    wide = P(("groups", "seq"), None)
    placed = (wide, shard, P(), P(), P(), P(), shard, P(), P(), P(), P(), P())
    return jax.shard_map(
        on_device, mesh=mesh, in_specs=placed, out_specs=(wide, wide), check_vma=False
    )
```

```python
import functools

import jax
import jax.numpy as jnp
import numpy as np
from jax import lax
from jax.experimental import pallas as pl
from jax.experimental.pallas import tpu as pltpu
from jax.sharding import PartitionSpec as P

MESH = pl.DeviceIdType.MESH
F32 = jnp.float32
BF16 = jnp.bfloat16
SUB = 8
LANES = 128


def dft_tables(rows):
    freq = (np.arange(rows) + 0.5)[:, None]
    angle = freq * np.arange(rows)[None, :] * (np.pi / rows)
    cos, sin = np.cos(angle), np.sin(angle)
    sign = np.where(np.arange(rows) % 2 == 0, 1.0, -1.0)[:, None]
    own = np.concatenate([cos, sin], 0)
    behind = np.concatenate([sign * sin, -sign * cos], 0)
    back = own.T / rows
    return [jnp.asarray(t, F32).astype(BF16) for t in (own, behind, back)]


def dot(left, right):
    return jnp.dot(left, right, preferred_element_type=F32)


def split(value):
    high = value.astype(BF16)
    return high, (value - high.astype(F32)).astype(BF16)


def one_minus_exp(a):
    series = 1.0 - a / 9.0
    for k in (8.0, 7.0, 6.0, 5.0, 4.0, 3.0, 2.0):
        series = 1.0 - series * a / k
    return jnp.where(a < 0.5, a * series, 1.0 - jnp.exp(-a))


def column(row):
    rows = row.shape[1]
    eye = lax.broadcasted_iota(jnp.int32, (rows, rows), 0) == lax.broadcasted_iota(
        jnp.int32, (rows, rows), 1
    )
    return jnp.sum(jnp.where(eye, row, 0.0), axis=1, keepdims=True)


def scaled(tokens, scale, gain):
    return (tokens.astype(F32) * scale * gain).astype(BF16)


def spectral_product(data, filt):
    half = data.shape[0] // 2
    dc, ds, fc, fs = data[:half], data[half:], filt[:half], filt[half:]
    return jnp.concatenate([dc * fc - ds * fs, dc * fs + ds * fc], 0).astype(BF16)


def modes_over_rows(first, step, out_ref):
    rows, width = out_ref.shape
    for lane in range(0, width, LANES):
        cols = slice(lane, lane + LANES)
        term, ratio = first[:, :, cols], step[:, :, cols]
        for a in range(rows // SUB):
            out_ref[a * SUB : (a + 1) * SUB, cols] = jnp.sum(term, axis=0)
            if a + 1 < rows // SUB:
                term = term * ratio


def end_state(signal_ref, step, last):
    rows, width = signal_ref.shape
    parts = []
    for lane in range(0, width, LANES):
        cols = slice(lane, lane + LANES)
        ratio = step[:, :, cols]
        total = jnp.broadcast_to(signal_ref[0:SUB, cols][None], ratio.shape)
        for a in range(1, rows // SUB):
            total = total * ratio + signal_ref[a * SUB : (a + 1) * SUB, cols][None]
        parts.append(jnp.sum(total * last[:, :, cols], axis=1))
    return jnp.concatenate(parts, 1)


def plane_size(n):
    size = 1
    while n % (2 * size) == 0 and 4 * size * size <= n:
        size *= 2
    return size


def hand_out(a_ref, b_ref, pa_ref, pb_ref, sem):
    copies = [
        pltpu.make_async_copy(a_ref, pa_ref, sem.at[0]),
        pltpu.make_async_copy(b_ref, pb_ref, sem.at[1]),
    ]
    for copy in copies:
        copy.start()
    for copy in copies:
        copy.wait()


def kernel(n, *refs):
    hbm = refs[:15]
    pa_ref, pb_ref = refs[15:17]
    vm = refs[17:32]
    (product_ref, rim_ref, filt_ref, signal_ref, carry_ref, state_ref, states_ref) = refs[32:39]
    (load_sem, rim_send, rim_recv, st_send, st_recv, far_sem) = refs[39:]
    me = lax.axis_index("seq")
    rows, width = vm[0].shape
    modes = vm[9].shape[0]

    plane = plane_size(n)
    planes = n // plane
    level, place = me // plane, lax.rem(me, plane)
    barrier = pltpu.get_barrier_semaphore()

    def signal(sem, target):
        pl.semaphore_signal(sem, inc=1, device_id={"seq": target}, device_id_type=MESH)

    @pl.loop(1, plane)
    def _(i):
        signal(barrier, level * plane + lax.rem(place + i, plane))

    @pl.loop(level + 1, planes)
    def _(i):
        signal(barrier, i * plane + place)

    @pl.when(jnp.logical_and(place == 0, level > 0))
    def _():
        signal(barrier, me - 1)

    loads = [pltpu.make_async_copy(h, v, load_sem.at[i]) for i, (h, v) in enumerate(zip(hbm, vm))]
    order = (0, 1, 2, 3, 12, 4, 9, 10, 13, 14, 5, 6, 7, 8, 11)
    for i in order:
        loads[i].start()
    (tok, rms_a, gain_a, proj_a, taps, out_a) = vm[:6]
    (rms_b, gain_b, proj_b, rates_ref, resid_ref, out_b, own_f, rim_f, back_f) = vm[6:]

    crossing = jnp.logical_and(place == plane - 1, level < planes - 1)

    def meet(count):
        pl.semaphore_wait(barrier, count)

        @pl.loop(0, level)
        def _(i):
            signal(far_sem, i * plane + place)

    @pl.when(jnp.logical_not(crossing))
    def _():
        meet(plane - 1 + level)

    for i in (0, 1, 2, 3):
        loads[i].wait()
    normed = scaled(tok[...], column(rms_a[...]), gain_a[...])
    projected = dot(normed, proj_a[...])
    queries = projected[:, :width]
    product = (projected[:, width : 2 * width] * projected[:, 2 * width :]).astype(BF16)
    product_ref[...] = product

    @pl.when(crossing)
    def _():
        meet(plane + level)

    rim_copy = pltpu.make_async_remote_copy(
        src_ref=product_ref,
        dst_ref=rim_ref,
        send_sem=rim_send,
        recv_sem=rim_recv,
        device_id={"seq": lax.rem(me + 1, n)},
        device_id_type=MESH,
    )

    @pl.when(me < n - 1)
    def _():
        rim_copy.start()

    loads[12].wait()
    loads[4].wait()
    spectrum = dot(own_f[...], product)
    taps_spec = dot(own_f[...], taps[...])

    loads[9].wait()
    loads[10].wait()
    rates = rates_ref[...]
    length = float(n * rows)
    weights = resid_ref[...] * jnp.sqrt(
        one_minus_exp(2.0 * rates) / one_minus_exp(2.0 * rates * length)
    )
    rates3 = jnp.broadcast_to(rates[:, None, :], (modes, SUB, width))
    within = lax.broadcasted_iota(jnp.int32, (modes, SUB, width), 1).astype(F32)
    step = jnp.exp(-rates3 * float(SUB))
    lag = jnp.exp(-rates3 * within)
    last = jnp.exp(-rates3 * (SUB - 1.0 - within))
    read = jnp.exp(-rates3 * (within + 1.0))
    block = jnp.exp(-rates * float(rows))
    modes_over_rows(weights[:, None, :] * lag, step, filt_ref)
    high, low = split(filt_ref[...])
    long_spec = dot(own_f[...], high) + dot(own_f[...], low)
    for i in (13, 14, 5, 6, 7, 8, 11):
        loads[i].wait()
    scale_b = column(rms_b[...])

    @pl.when(me > 0)
    def _():
        rim_copy.wait_recv()
        carry_ref[...] = dot(rim_f[...], rim_ref[...])

    @pl.when(me == 0)
    def _():
        carry_ref[...] = jnp.zeros_like(carry_ref)

    short_out = dot(back_f[...], spectral_product(spectrum + carry_ref[...], taps_spec))
    gated_a = (queries * short_out).astype(BF16)
    partial_a = dot(gated_a, out_a[...]).astype(BF16)
    pa_ref[...] = partial_a
    hidden = (tok[...].astype(F32) + partial_a.astype(F32)).astype(BF16)
    normed_b = scaled(hidden, scale_b, gain_b[...])
    pair_b = dot(normed_b, proj_b[:, width:])
    signal = (pair_b[:, :width] * pair_b[:, width:]).astype(BF16)
    signal_ref[...] = signal.astype(F32)
    state_ref[...] = end_state(signal_ref, step, last).astype(BF16)

    def state_copy(source, target):
        return pltpu.make_async_remote_copy(
            src_ref=state_ref,
            dst_ref=states_ref.at[source],
            send_sem=st_send.at[target],
            recv_sem=st_recv.at[source],
            device_id={"seq": target},
            device_id_type=MESH,
        )

    @pl.loop(me + 1, (level + 1) * plane)
    def _(target):
        state_copy(me, target).start()

    @pl.when(level < planes - 1)
    def _():
        pl.semaphore_wait(far_sem, planes - 1 - level)

    @pl.loop(0, plane)
    def _(i):
        @pl.loop(0, planes - 1 - level)
        def _(k):
            state_copy(me, (planes - 1 - k) * plane + i).start()


    queries_b = dot(normed_b, proj_b[:, :width])
    local = dot(back_f[...], spectral_product(dot(own_f[...], signal), long_spec))

    def gather(source, total):
        state_copy(source, lax.rem(me + 1, n)).wait_recv()
        return total * block + states_ref[source].astype(F32)

    total = lax.fori_loop(0, me, gather, jnp.zeros((modes, width), F32))
    modes_over_rows((total * weights)[:, None, :] * read, step, filt_ref)
    long_out = (local + filt_ref[...]).astype(BF16)
    gated_b = (queries_b * long_out.astype(F32)).astype(BF16)
    pb_ref[...] = dot(gated_b, out_b[...]).astype(BF16)

    @pl.when(me < n - 1)
    def _():
        rim_copy.wait_send()

    @pl.loop(0, n - 1 - me)
    def _(i):
        state_copy(me, n - 1 - i).wait_send()


def solution(mesh):
    n = mesh.shape["seq"]

    def on_device(*args):
        rows, width = args[0].shape
        modes = args[9].shape[0]
        args = [a[None] if a.ndim == 1 else a for a in args] + dft_tables(rows)
        block = jax.ShapeDtypeStruct((rows, width), BF16)
        fast = pltpu.VMEM((rows, width), BF16)
        inside = pl.BlockSpec(memory_space=pltpu.VMEM)
        anywhere = pl.BlockSpec(memory_space=pl.ANY)
        results = pl.pallas_call(
            functools.partial(kernel, n),
            out_shape=(fast, fast),
            in_specs=[anywhere] * len(args),
            out_specs=(inside, inside),
            scratch_shapes=[pltpu.VMEM(a.shape, a.dtype) for a in args]
            + [
                pltpu.VMEM((rows, width), BF16),
                pltpu.VMEM((rows, width), BF16),
                pltpu.VMEM((rows, width), F32),
                pltpu.VMEM((rows, width), F32),
                pltpu.VMEM((2 * rows, width), F32),
                pltpu.VMEM((modes, width), BF16),
                pltpu.VMEM((n, modes, width), BF16),
                pltpu.SemaphoreType.DMA((len(args),)),
                pltpu.SemaphoreType.DMA,
                pltpu.SemaphoreType.DMA,
                pltpu.SemaphoreType.DMA((n,)),
                pltpu.SemaphoreType.DMA((n,)),
                pltpu.SemaphoreType.REGULAR,
            ],
            compiler_params=pltpu.CompilerParams(collective_id=0, has_side_effects=True),
        )(*args)
        return pl.pallas_call(
            hand_out,
            out_shape=(block, block),
            in_specs=[inside] * 2,
            out_specs=(anywhere, anywhere),
            scratch_shapes=[pltpu.SemaphoreType.DMA((2,))],
        )(*[pltpu.with_memory_space_constraint(r, pltpu.VMEM) for r in results])

    shard = P(("groups", "seq"))
    wide = P(("groups", "seq"), None)
    placed = (wide, shard, P(), P(), P(), P(), shard, P(), P(), P(), P(), P())
    return jax.shard_map(
        on_device, mesh=mesh, in_specs=placed, out_specs=(wide, wide), check_vma=False
    )
```
